32 devices in a mesh: dp: 16 (over z, y, core), mp: 2 (over x).
Axes of the slice: x: 2, y: 2, z: 4, core: 2. Of those that a mesh axis runs over, the one named last changes fastest.
Arguments:
- layer_input: bfloat16 [2, 16, 256, 2048], P(None, 'dp', 'mp')
- out_grad: bfloat16 [2, 16, 256, 2048], P(None, 'dp', 'mp')
- valid_count: int32 [2, 16], P(None, 'dp'), may hold values from 129 to 256, as said below
- w_query: bfloat16 [2048, 2048], P('dp', 'mp'), may hold values from -0.125 to 0.125
- w_key: bfloat16 [2048, 2048], P('dp', 'mp'), may hold values from -0.125 to 0.125
- w_value: bfloat16 [2048, 2048], P('dp', 'mp'), may hold values from -0.125 to 0.125
- w_output: bfloat16 [2048, 2048], P('dp', 'mp'), may hold values from -0.75 to 0.75
- w_gate: bfloat16 [2048, 8192], P('dp', 'mp'), may hold values from -0.125 to 0.125
- w_up: bfloat16 [2048, 8192], P('dp', 'mp'), may hold values from -0.125 to 0.125
- w_down: bfloat16 [2048, 8192], P('dp', 'mp'), may hold values from -0.0625 to 0.0625
- gain_attn: float32 [2048], replicated, may hold values from 0.5 to 1.5
- gain_mlp: float32 [2048], replicated, may hold values from 0.5 to 1.5
- memory_gate: float32 [16], replicated, may hold values from -3 to 3
Outputs:
- layer_output: bfloat16 [2, 16, 256, 2048], P(None, 'dp', 'mp')
- grad_input: float32 [2, 16, 256, 2048], P(None, 'dp', 'mp')
- grad_query: float32 [2048, 2048], P('dp', 'mp')
- grad_key: float32 [2048, 2048], P('dp', 'mp')
- grad_value: float32 [2048, 2048], P('dp', 'mp')
- grad_output: float32 [2048, 2048], P('dp', 'mp')
- grad_gate: float32 [2048, 8192], P('dp', 'mp')
- grad_up: float32 [2048, 8192], P('dp', 'mp')
- grad_down: float32 [2048, 8192], P('dp', 'mp')
- grad_norm_attn: float32 [2048], replicated
- grad_norm_mlp: float32 [2048], replicated
- grad_memory_gate: float32 [16], replicated
The draws below stay inside these ranges and needn't reach their ends.
Inputs may be any that keep to these rules, and one draw needn't show every extreme that they name: valid_count counts the valid leading tokens of each sequence; its first segment is always full and some sequence is full to 256.
All inputs are finite; a program needn't handle non-finite values.
Results may differ from the reference program's by a relative error of at most 0.014.
Values may be sent and summed in bfloat16 or wider, within the bound.
No kernel may reach another device: no remote copies, remote signals or barrier semaphores. Data moves between devices by JAX's collectives and lax.ppermute only.
A program may use at most 448 MiB of HBM per device.

```python
import math
import jax
import jax.numpy as jnp
from jax import lax

D = 2048
H = 16
HD = 128
FF = 8192
SEG = 128
LEN = 256
MB = 2
SEQS = 16


def draw_layer_input(key, part):
    key_main, key_rows, key_cols = jax.random.split(key, 3)
    normal_part = jax.random.normal(key_main, (MB, SEQS, LEN, D), jnp.float32)
    row_scale = jnp.exp(jax.random.uniform(key_rows, (MB, SEQS, LEN, 1), jnp.float32, math.log(0.3), math.log(3.0)))
    col_scale = jnp.exp(jax.random.uniform(key_cols, (D,), jnp.float32, math.log(0.3), math.log(3.0)))
    return (normal_part * row_scale * col_scale).astype(jnp.bfloat16)


def draw_out_grad(key, part):
    key_noise = jax.random.fold_in(key, 0)
    rising = 1.0 + 2.0 * jnp.arange(SEQS, dtype=jnp.float32).reshape(1, SEQS, 1, 1) / max(SEQS - 1, 1)
    noise = jax.random.normal(key_noise, (MB, SEQS, LEN, D), jnp.float32)
    return (noise * rising).astype(jnp.bfloat16)


def draw_valid_count(key, part):
    key_counts, key_full = jax.random.split(key, 2)
    counts = jax.random.randint(key_counts, (MB * SEQS,), SEG + 1, LEN + 1)
    full_at = jax.random.randint(key_full, (), 0, MB * SEQS)
    counts = jnp.where(jnp.arange(MB * SEQS) == full_at, LEN, counts)
    return counts.reshape(MB, SEQS).astype(jnp.int32)


def shard_levels(stream_key, extent, cuts, low, largest):
    def one(dim, blocks):
        steps = jax.random.uniform(jax.random.fold_in(jax.random.fold_in(stream_key, 6), dim), (blocks,), jnp.float32, low / len(cuts), largest / len(cuts))
        return jnp.repeat(jnp.exp(steps), extent[dim] // blocks).reshape((-1,) + (1,) * (len(extent) - dim - 1))

    gain = one(*cuts[0])
    for cut in cuts[1:]:
        gain = gain * one(*cut)
    return gain


def normal_values(key, shape, scale, limit, cuts=(), held_as=jnp.bfloat16):
    entries = scale * jax.random.normal(key, shape, jnp.float32)
    if cuts:
        entries = entries * shard_levels(key, shape, cuts, -0.22, 0.18)
    return jnp.clip(entries, -limit, limit).astype(held_as)


def setup_inputs(seed: int = 0) -> dict:
    streams_of = jax.random.split(jax.random.key(seed), 14)
    return {
        "layer_input": draw_layer_input(jax.random.fold_in(streams_of[13], 71), 0),
        "out_grad": draw_out_grad(jax.random.fold_in(streams_of[13], 71), 0),
        "valid_count": draw_valid_count(jax.random.fold_in(streams_of[13], 71), 0),
        "w_query": normal_values(streams_of[3], (D, D), D ** -0.5, 0.125, ((0, 16), (1, 2))),
        "w_key": normal_values(streams_of[4], (D, D), D ** -0.5, 0.125, ((0, 16), (1, 2))),
        "w_value": normal_values(streams_of[5], (D, D), D ** -0.5, 0.125, ((0, 16), (1, 2))),
        "w_output": normal_values(streams_of[6], (D, D), (D // 32) ** -0.5, 0.75, ((0, 16), (1, 2))),
        "w_gate": normal_values(streams_of[7], (D, FF), D ** -0.5, 0.125, ((0, 16), (1, 2))),
        "w_up": normal_values(streams_of[8], (D, FF), D ** -0.5, 0.125, ((0, 16), (1, 2))),
        "w_down": normal_values(streams_of[9], (D, FF), FF ** -0.5, 0.0625, ((0, 16), (1, 2))),
        "gain_attn": jnp.clip(1.0 + 0.1 * jax.random.normal(streams_of[10], (D,), jnp.float32), 0.5, 1.5),
        "gain_mlp": jnp.clip(1.0 + 0.1 * jax.random.normal(streams_of[11], (D,), jnp.float32), 0.5, 1.5),
        "memory_gate": jnp.clip(jax.random.uniform(streams_of[12], (H,), jnp.float32, -3.0, 3.0), -3.0, 3.0),
    }


epsilon = 1e-05
masked_score = -1e+30
highest = lax.Precision.HIGHEST

@jax.custom_vjp
def low(v):
    return lax.optimization_barrier(v.astype(jnp.bfloat16)).astype(jnp.float32)

@jax.custom_vjp
def low_back(v):
    return v

def low_keep(v):
    return (low(v), None)

def low_pass(kept, grad):
    return (grad,)

def back_keep(v):
    return (v, None)

def back_low(kept, grad):
    return (low(grad),)
low.defvjp(low_keep, low_pass)
low_back.defvjp(back_keep, back_low)

def project(inputs, weight):
    return jnp.einsum('btd,dc->btc', inputs, weight, precision=highest)

def positive_map(values):
    return jnp.where(values > 0.0, values + 1.0, jnp.exp(jnp.minimum(values, 0.0)))

def block_forward(inputs, w_query, w_key, w_value, w_output, w_gate, w_up, w_down, gain_attn, gain_mlp, memory_gate, valid_rows):
    seq_count = inputs.shape[0]
    inv_first = lax.rsqrt(lax.optimization_barrier(jnp.mean(inputs * inputs, axis=-1, keepdims=True)) + epsilon)
    normed = low(inputs * inv_first * gain_attn)
    queries = low_back(low(project(normed, w_query))).reshape(seq_count, 2, SEG, H, HD)
    key_rows = low_back(low(project(normed, w_key))).reshape(seq_count, 2, SEG, H, HD)
    value_rows = low_back(low(project(normed, w_value))).reshape(seq_count, 2, SEG, H, HD)
    score_scale = HD ** (-0.5)
    scores = low_back(jnp.einsum('bnqhe,bnkhe->bnhqk', queries, key_rows, precision=highest) * score_scale)
    position = jnp.arange(SEG)
    causal = position[:, None] >= position[None, :]
    key_valid = valid_rows.reshape(seq_count, 2, 1, 1, SEG) > 0.5
    scores = jnp.where(causal & key_valid, scores, masked_score)
    top_score = lax.optimization_barrier(jnp.max(scores, axis=-1, keepdims=True))
    exponent = jnp.exp(scores - top_score)
    probability = exponent / lax.optimization_barrier(jnp.sum(exponent, axis=-1, keepdims=True))
    local_out = low_back(jnp.einsum('bnhqk,bnkhe->bnqhe', low(probability), value_rows, precision=highest))
    query_map = low(positive_map(queries[:, 1]))
    key_map = low(positive_map(key_rows[:, 0])) * valid_rows[:, :SEG].reshape(seq_count, SEG, 1, 1)
    memory = low_back(low(jnp.einsum('bthe,bthf->bhef', key_map, value_rows[:, 0], precision=highest)))
    normalizer = lax.optimization_barrier(jnp.sum(key_map, axis=1))
    numerator = low_back(jnp.einsum('bthe,bhef->bthf', query_map, memory, precision=highest))
    denominator = jnp.einsum('bthe,bhe->bth', query_map, normalizer, precision=highest)
    retrieved = numerator / denominator[..., None]
    gate_value = jax.nn.sigmoid(memory_gate)[:, None]
    first_seg = (1.0 - gate_value) * local_out[:, 0]
    second = gate_value * retrieved + (1.0 - gate_value) * local_out[:, 1]
    combined = jnp.stack([first_seg, second], axis=1).reshape(seq_count, LEN, D)
    heads_out = low(combined * valid_rows[..., None])
    attn_out = low_back(jnp.einsum('btc,dc->btd', heads_out, w_output, precision=highest))
    hidden_state = inputs + attn_out
    inv_second = lax.rsqrt(lax.optimization_barrier(jnp.mean(hidden_state * hidden_state, axis=-1, keepdims=True)) + epsilon)
    normed_mlp = low(hidden_state * inv_second * gain_mlp)
    gate_pre = low_back(project(normed_mlp, w_gate))
    up_pre = low_back(project(normed_mlp, w_up))
    activated = low(gate_pre * jax.nn.sigmoid(gate_pre) * up_pre)
    mlp_out = jnp.einsum('btf,df->btd', activated, w_down, precision=highest)
    return hidden_state + mlp_out

def reference(layer_input, out_grad, valid_count, w_query, w_key, w_value, w_output, w_gate, w_up, w_down, gain_attn, gain_mlp, memory_gate):
    group_size = math.gcd(SEQS, max(1, 4096 // LEN))
    blocks = MB * SEQS // group_size
    inputs = layer_input.astype(jnp.float32).reshape(blocks, group_size, LEN, D)
    cotangent = out_grad.astype(jnp.float32).reshape(blocks, group_size, LEN, D)
    counts = valid_count.reshape(blocks, group_size)
    params = tuple((weight.astype(jnp.float32) for weight in (w_query, w_key, w_value, w_output, w_gate, w_up, w_down))) + (gain_attn, gain_mlp, memory_gate)

    def one_block(carried, scanned):
        piece_in, piece_grad, piece_count = scanned
        valid_rows = (jnp.arange(LEN)[None, :] < piece_count[:, None]).astype(jnp.float32)

        def forward(inputs_here, *weights):
            return block_forward(inputs_here, *weights, valid_rows)
        result, pullback = jax.vjp(forward, piece_in, *params)
        gradients = pullback(piece_grad)
        new_carry = tuple((running + addend for running, addend in zip(carried, gradients[1:])))
        return (new_carry, (result.astype(jnp.bfloat16), gradients[0]))
    zeros_start = tuple((jnp.zeros_like(weight) for weight in params))
    totals, (outputs, input_grads) = lax.scan(one_block, zeros_start, (inputs, cotangent, counts))
    return (outputs.reshape(MB, SEQS, LEN, D), input_grads.reshape(MB, SEQS, LEN, D), totals[0], totals[1], totals[2], totals[3], totals[4], totals[5], totals[6], totals[7], totals[8], totals[9])
```

```python
import jax
import jax.numpy as jnp
from jax import lax
from jax.sharding import PartitionSpec as P

HD = 128
MLP_CHUNKS = 4


epsilon = 1e-05
masked_score = -1e30
f32 = jnp.float32
bf16 = jnp.bfloat16


def positive_map(values):
    return jnp.where(values > 0.0, values + 1.0, jnp.exp(jnp.minimum(values, 0.0)))


def positive_slope(values):
    return jnp.where(values > 0.0, 1.0, jnp.exp(jnp.minimum(values, 0.0)))


def fold_weights(inputs, weight):
    return jnp.dot(inputs, weight, preferred_element_type=f32)


def map_weights(inputs, weight):
    return lax.dot_general(inputs, weight, (((1,), (1,)), ((), ())), preferred_element_type=f32)


def row_product(left, right):
    return lax.dot_general(left, right, (((0,), (0,)), ((), ())), preferred_element_type=f32)


class Place:
    def __init__(self, dp_size):
        self.size = dp_size
        self.line = dp_size // 4
        index = lax.axis_index("dp")
        self.core = index % 2
        self.side = (index // 2) % 2
        self.pos = index // 4
        self.half = lax.axis_index("mp")

    def swap_core(self, value):
        return lax.ppermute(value, "dp", [(i, i ^ 1) for i in range(self.size)])

    def swap_side(self, value):
        return lax.ppermute(value, "dp", [(i, i ^ 2) for i in range(self.size)])

    def rotate(self, value, step):
        pairs = [(i, (i + 4 * step) % self.size) for i in range(self.size)]
        return lax.ppermute(value, "dp", pairs)

    def swap_half(self, value):
        return lax.ppermute(value, "mp", [(0, 1), (1, 0)])

    def order_line(self, blocks, axis):
        out = jnp.roll(jnp.flip(blocks, axis), 1, axis)
        step = 1
        while step < self.line:
            out = jnp.where((self.pos // step) % 2 == 1, jnp.roll(out, step, axis), out)
            step *= 2
        return out

    def order_side(self, blocks, axis):
        return jnp.where(self.side == 1, jnp.flip(blocks, axis), blocks)

    def to_local(self, value):
        lead = value.shape[:-1]
        axis = len(lead)
        blocks = value.reshape(lead + (self.line, 2, -1))
        blocks = self.order_side(self.order_line(blocks, axis), axis + 1)
        return jnp.swapaxes(blocks, axis, axis + 1).reshape(value.shape)

    def to_global(self, value):
        lead = value.shape[:-1]
        axis = len(lead)
        blocks = jnp.swapaxes(value.reshape(lead + (2, self.line, -1)), axis, axis + 1)
        blocks = self.order_side(self.order_line(blocks, axis), axis + 1)
        return blocks.reshape(value.shape)

    def share_columns(self, weights):
        mine, other = [], []
        for weight in weights:
            width = weight.shape[1] // 2
            mine.append(lax.dynamic_slice_in_dim(weight, self.core * width, width, 1))
            other.append(lax.dynamic_slice_in_dim(weight, (1 - self.core) * width, width, 1))
        mine = jnp.concatenate(mine, axis=1)
        got = self.swap_core(jnp.concatenate(other, axis=1))
        first = jnp.where(self.core == 0, mine, got)
        second = jnp.where(self.core == 0, got, mine)
        return jnp.concatenate([first, second], axis=0)

    def gather_blocks(self, block):
        near = [block] + [self.rotate(block, step) for step in range(1, self.line)]
        return near + [self.swap_side(piece) for piece in near]

    def gather_rows(self, local):
        across = self.swap_half(local)
        near = jnp.where(self.half == 0, jnp.stack([local, across], 1), jnp.stack([across, local], 1))
        far = self.swap_core(near)
        seqs, _, tokens, width = near.shape
        return jnp.stack([near, far], 0).reshape(2, seqs, 2 * tokens, width)

    def reduce_rows(self, own, sibling, seqs, tokens):
        width = own.shape[1]
        total = own + self.swap_core(sibling.astype(bf16)).astype(f32)
        total = total.reshape(seqs, 2, tokens, width)
        keep = jnp.where(self.half == 0, total[:, 0], total[:, 1])
        send = jnp.where(self.half == 0, total[:, 1], total[:, 0]).astype(bf16)
        return keep + self.swap_half(send).astype(f32)

    def sum_all(self, value):
        step = 1
        while step < self.size:
            value = value + lax.ppermute(value, "dp", [(i, i ^ step) for i in range(self.size)])
            step *= 2
        return value + self.swap_half(value)

    def reduce_grad(self, left, right):
        rows = left.shape[1] // 2
        cols = right.shape[1]
        away = self.swap_side(row_product(left[:, rows:], right).astype(bf16))
        near = row_product(left[:, :rows], right)
        near = (near + away.astype(f32)).astype(bf16)
        size = rows // self.line
        total = near[:size].astype(f32)
        for step in range(1, self.line):
            piece = near[step * size : (step + 1) * size]
            total = total + self.rotate(piece, self.line - step).astype(f32)
        total = total.reshape(2, size // 2, cols)
        mine = jnp.where(self.core == 0, total[0], total[1])
        other = jnp.where(self.core == 0, total[1], total[0])
        got = self.swap_core(other)
        return jnp.where(self.core == 0, mine, got), jnp.where(self.core == 0, got, mine)


def attention(qkv_rows, counts, gate_local, seg_len):
    seqs = counts.shape[0]
    heads = gate_local.shape[0]
    attn_width = heads * HD
    full_len = 2 * seg_len
    total_rows = seqs * full_len
    shape_heads = (seqs, 2, seg_len, heads, HD)
    score_scale = HD ** (-0.5)
    valid_rows = (jnp.arange(full_len)[None, :] < counts[:, None]).astype(f32)
    queries = qkv_rows[:, :attn_width].reshape(shape_heads)
    key_rows = qkv_rows[:, attn_width : 2 * attn_width].reshape(shape_heads)
    value_rows = qkv_rows[:, 2 * attn_width :].reshape(shape_heads)
    raw_scores = (
        jnp.einsum("bnqhe,bnkhe->bnhqk", queries, key_rows, preferred_element_type=f32)
        * score_scale
    )
    seg_pos = jnp.arange(seg_len)
    causal = seg_pos[:, None] >= seg_pos[None, :]
    key_valid = valid_rows.reshape(seqs, 2, 1, 1, seg_len) > 0.5
    scores = jnp.where(causal & key_valid, raw_scores, masked_score)
    top_score = jnp.max(scores, axis=-1, keepdims=True)
    exponent = jnp.exp(scores - top_score)
    probability = exponent / jnp.sum(exponent, axis=-1, keepdims=True)
    prob_low = probability.astype(bf16)
    local_out = jnp.einsum("bnhqk,bnkhe->bnqhe", prob_low, value_rows, preferred_element_type=f32)
    query_map = positive_map(queries[:, 1].astype(f32)).astype(bf16)
    seg_valid = valid_rows[:, :seg_len].reshape(seqs, seg_len, 1, 1)
    key_map = positive_map(key_rows[:, 0].astype(f32)).astype(bf16).astype(f32) * seg_valid
    key_map_low = key_map.astype(bf16)
    memory = jnp.einsum("bthe,bthf->bhef", key_map_low, value_rows[:, 0], preferred_element_type=f32)
    memory_low = memory.astype(bf16)
    normalizer = jnp.sum(key_map, axis=1)
    numerator = jnp.einsum("bthe,bhef->bthf", query_map, memory_low, preferred_element_type=f32)
    denominator = jnp.sum(query_map.astype(f32) * normalizer[:, None], axis=-1)
    retrieved = numerator / denominator[..., None]
    gate_sig = jax.nn.sigmoid(gate_local)
    gate_value = gate_sig[:, None]
    first_seg = (1.0 - gate_value) * local_out[:, 0]
    second = gate_value * retrieved + (1.0 - gate_value) * local_out[:, 1]
    combined = jnp.stack([first_seg, second], axis=1).reshape(seqs, full_len, attn_width)
    heads_out = (combined * valid_rows[..., None]).astype(bf16).reshape(total_rows, attn_width)

    def backward(heads_grad):
        grad_comb = (
            heads_grad.reshape(seqs, full_len, attn_width) * valid_rows[..., None]
        ).reshape(shape_heads)
        gate_sum = jnp.sum(
            grad_comb[:, 0] * -local_out[:, 0] + grad_comb[:, 1] * (retrieved - local_out[:, 1]),
            axis=(0, 1, 3),
        )
        gate_part = gate_sum * gate_sig * (1.0 - gate_sig)
        local_back = ((1.0 - gate_value) * grad_comb).astype(bf16)
        retrieved_back = gate_value * grad_comb[:, 1]
        numer_back = (retrieved_back / denominator[..., None]).astype(bf16)
        denom_back = -jnp.sum(retrieved_back * numerator, axis=-1) / (denominator * denominator)
        prob_back = jnp.einsum(
            "bnqhe,bnkhe->bnhqk", local_back, value_rows, preferred_element_type=f32
        )
        value_back = jnp.einsum(
            "bnhqk,bnqhe->bnkhe", prob_low, local_back, preferred_element_type=f32
        )
        score_back = (
            probability * (prob_back - jnp.sum(prob_back * probability, axis=-1, keepdims=True))
        ).astype(bf16)
        query_back = (
            jnp.einsum("bnhqk,bnkhe->bnqhe", score_back, key_rows, preferred_element_type=f32)
            * score_scale
        )
        key_back = (
            jnp.einsum("bnhqk,bnqhe->bnkhe", score_back, queries, preferred_element_type=f32)
            * score_scale
        )
        memory_back = jnp.einsum(
            "bthe,bthf->bhef", query_map, numer_back, preferred_element_type=f32
        ).astype(bf16)
        qmap_back = (
            jnp.einsum("bthf,bhef->bthe", numer_back, memory_low, preferred_element_type=f32)
            + denom_back[..., None] * normalizer[:, None]
        )
        norm_back = jnp.sum(denom_back[..., None] * query_map.astype(f32), axis=1)
        kmap_back = (
            jnp.einsum("bthf,bhef->bthe", value_rows[:, 0], memory_back, preferred_element_type=f32)
            + norm_back[:, None]
        ) * seg_valid
        value_from_memory = jnp.einsum(
            "bthe,bhef->bthf", key_map_low, memory_back, preferred_element_type=f32
        )
        query_back = query_back.at[:, 1].add(
            qmap_back * positive_slope(queries[:, 1].astype(f32))
        )
        key_back = key_back.at[:, 0].add(kmap_back * positive_slope(key_rows[:, 0].astype(f32)))
        value_back = value_back.at[:, 0].add(value_from_memory)
        grad_qkv = jnp.concatenate(
            [
                query_back.reshape(total_rows, attn_width).astype(bf16),
                key_back.reshape(total_rows, attn_width).astype(bf16),
                value_back.reshape(total_rows, attn_width).astype(bf16),
            ],
            axis=1,
        )
        return grad_qkv, gate_part

    return heads_out, backward


def join(blocks, start, stop):
    return jnp.concatenate([block[:, start:stop] for block in blocks], axis=0)


def on_device(
    dp_size,
    layer_input,
    out_grad,
    valid_count,
    w_query,
    w_key,
    w_value,
    w_output,
    w_gate,
    w_up,
    w_down,
    gain_attn,
    gain_mlp,
    memory_gate,
):
    place = Place(dp_size)
    micros, seqs_each, tokens, width = layer_input.shape
    seqs = micros * seqs_each
    rows_half = seqs * 2 * tokens
    heads_local = w_query.shape[1] // HD // 2
    attn_width = heads_local * HD
    ff_width = w_gate.shape[1] // 2
    chunk = ff_width // MLP_CHUNKS
    head_start = (place.half * 2 + place.core) * heads_local
    gate_local = lax.dynamic_slice_in_dim(memory_gate, head_start, heads_local, 0)

    qkv_block = place.share_columns([w_query, w_key, w_value])
    out_block = place.share_columns([w_output])
    mlp_block = place.share_columns([w_gate, w_up, w_down])
    qkv_blocks = place.gather_blocks(qkv_block)
    out_blocks = place.gather_blocks(out_block)
    mlp_blocks = []
    for part in range(MLP_CHUNKS):
        start = part * chunk
        mlp_blocks.append(
            place.gather_blocks(
                jnp.concatenate(
                    [mlp_block[:, i * ff_width + start : i * ff_width + start + chunk] for i in range(3)],
                    axis=1,
                )
            )
        )

    inputs = place.to_local(layer_input.reshape(seqs, tokens, width)).astype(f32)
    local_grad = place.to_local(out_grad.reshape(seqs, tokens, width))
    gain_attn_l = place.to_local(gain_attn)
    gain_mlp_l = place.to_local(gain_mlp)
    own_counts = valid_count.reshape(seqs).astype(f32)
    counts = jnp.concatenate([own_counts, place.swap_core(own_counts)]).astype(jnp.int32)

    inv_first = lax.rsqrt(jnp.mean(inputs * inputs, axis=-1, keepdims=True) + epsilon)
    normed = (inputs * inv_first * gain_attn_l).astype(bf16)
    normed_all = place.gather_rows(normed).reshape(2 * rows_half, width)
    w_qkv = join(qkv_blocks, 0, 3 * attn_width)
    qkv_rows = fold_weights(normed_all, w_qkv).astype(bf16)
    heads_out, attention_back = attention(qkv_rows, counts, gate_local, tokens)
    w_out = join(out_blocks, 0, attn_width)
    attn_out = place.reduce_rows(
        map_weights(heads_out[:rows_half], w_out),
        map_weights(heads_out[rows_half:], w_out),
        seqs,
        tokens,
    )
    hidden_state = inputs + attn_out
    inv_second = lax.rsqrt(jnp.mean(hidden_state * hidden_state, axis=-1, keepdims=True) + epsilon)
    normed_mlp = (hidden_state * inv_second * gain_mlp_l).astype(bf16)
    mlp_in = place.gather_rows(normed_mlp).reshape(2 * rows_half, width)
    grad_rows = place.gather_rows(local_grad).reshape(2 * rows_half, width)

    out_own = out_sib = back_own = back_sib = 0.0
    grads_gate, grads_up, grads_down = [], [], []
    for part in range(MLP_CHUNKS):
        w_gu = join(mlp_blocks[part], 0, 2 * chunk)
        w_dn = join(mlp_blocks[part], 2 * chunk, 3 * chunk)
        gate_up = fold_weights(mlp_in, w_gu)
        gate_pre = gate_up[:, :chunk]
        up_pre = gate_up[:, chunk:]
        sigma = jax.nn.sigmoid(gate_pre)
        activated = (gate_pre * sigma * up_pre).astype(bf16)
        act_back = fold_weights(grad_rows, w_dn)
        gate_back = (act_back * up_pre * sigma * (1.0 + gate_pre * (1.0 - sigma))).astype(bf16)
        up_back = (act_back * gate_pre * sigma).astype(bf16)
        grad_gu = jnp.concatenate([gate_back, up_back], axis=1)
        back_sib = back_sib + map_weights(grad_gu[rows_half:], w_gu)
        back_own = back_own + map_weights(grad_gu[:rows_half], w_gu)
        out_sib = out_sib + map_weights(activated[rows_half:], w_dn)
        out_own = out_own + map_weights(activated[:rows_half], w_dn)
        pair_gu = place.reduce_grad(mlp_in, grad_gu)
        pair_dn = place.reduce_grad(grad_rows, activated)
        grads_gate.append([value[:, :chunk] for value in pair_gu])
        grads_up.append([value[:, chunk:] for value in pair_gu])
        grads_down.append(pair_dn)

    mlp_back = place.reduce_rows(back_own, back_sib, seqs, tokens)
    mlp_out = place.reduce_rows(out_own, out_sib, seqs, tokens)
    layer_out = (hidden_state + mlp_out).astype(bf16)
    scaled_mlp = mlp_back * gain_mlp_l
    hidden_back = local_grad.astype(f32) + inv_second * (
        scaled_mlp
        - hidden_state
        * inv_second
        * inv_second
        * jnp.mean(scaled_mlp * hidden_state, axis=-1, keepdims=True)
    )
    gain_mlp_part = jnp.sum(mlp_back * hidden_state * inv_second, axis=(0, 1))
    hidden_rows = place.gather_rows(hidden_back.astype(bf16)).reshape(2 * rows_half, width)
    grad_out_pair = place.reduce_grad(hidden_rows, heads_out)
    grad_qkv, gate_part = attention_back(fold_weights(hidden_rows, w_out))
    attn_back = place.reduce_rows(
        map_weights(grad_qkv[:rows_half], w_qkv),
        map_weights(grad_qkv[rows_half:], w_qkv),
        seqs,
        tokens,
    )
    grad_qkv_pair = place.reduce_grad(normed_all, grad_qkv)
    scaled_attn = attn_back * gain_attn_l
    grad_input = hidden_back + inv_first * (
        scaled_attn
        - inputs * inv_first * inv_first * jnp.mean(scaled_attn * inputs, axis=-1, keepdims=True)
    )
    gain_attn_part = jnp.sum(attn_back * inputs * inv_first, axis=(0, 1))

    gate_full = lax.dynamic_update_slice_in_dim(
        jnp.zeros((memory_gate.shape[0],), f32), gate_part, head_start, 0
    )
    sums = place.sum_all(
        jnp.concatenate(
            [place.to_global(gain_attn_part), place.to_global(gain_mlp_part), gate_full]
        )
    )

    def whole(index):
        return jnp.concatenate(
            [side[:, index * attn_width : (index + 1) * attn_width] for side in grad_qkv_pair], axis=1
        )

    def chunks(pieces):
        return jnp.concatenate([piece[side] for side in range(2) for piece in pieces], axis=1)

    shape = (micros, seqs_each, tokens, width)
    return (
        place.to_global(layer_out).reshape(shape),
        place.to_global(grad_input).reshape(shape),
        whole(0),
        whole(1),
        whole(2),
        jnp.concatenate(grad_out_pair, axis=1),
        chunks(grads_gate),
        chunks(grads_up),
        chunks(grads_down),
        sums[:width],
        sums[width : 2 * width],
        sums[2 * width :],
    )


def solution(mesh):
    rows = P(None, "dp", "mp", None)
    weight = P("dp", "mp")
    dp_size = mesh.shape["dp"]

    def run(*args):
        return on_device(dp_size, *args)

    return jax.shard_map(
        run,
        mesh=mesh,
        in_specs=(rows, rows, P(None, "dp")) + (weight,) * 7 + (P(), P(), P()),
        out_specs=(rows, rows) + (weight,) * 7 + (P(), P(), P()),
        check_vma=False,
    )
```
